32 devices in a mesh: dp: 2 (over x), expert: 16 (over z, y, core).
Axes of the slice: x: 2, y: 2, z: 4, core: 2. Of those that a mesh axis runs over, the one named last changes fastest.
Arguments:
- saved_inputs: bfloat16 [1024, 3584], P('expert'), may hold values from -6 to 6
- output_grad: bfloat16 [1024, 3584], P('expert'), may hold values from -6 to 6
- routes: int32 [1024, 8], P('expert'), may hold values from 0 to 15, all different within a row; in each aligned block of 64 rows (0 to 63, 64 to 127, ...) at most 36 rows name the same one
- route_gates: bfloat16 [1024, 8], P('expert'), may hold values from 0.099609375 to 1
- expert_gate: bfloat16 [16, 3584, 1024], P('expert', None, 'dp'), may hold values from -0.09375 to 0.09375
- expert_up: bfloat16 [16, 3584, 1024], P('expert', None, 'dp'), may hold values from -0.09375 to 0.09375
- expert_down: bfloat16 [16, 1024, 3584], P('expert', 'dp'), may hold values from -0.1875 to 0.1875
- proj_basis: bfloat16 [16, 1024, 128], P('expert', 'dp'), may hold values from -0.1875 to 0.1875
Outputs:
- input_grad: bfloat16 [1024, 3584], P('expert', 'dp')
- projected: float32 [16, 3584, 3, 128], P('expert', 'dp')
The draws below stay inside these ranges and needn't reach their ends.
Inputs may be any that keep to these rules, and one draw needn't show every extreme that they name: Within each aligned block of 64 tokens no expert is named by more than 36 routes, and in every draw some expert is named by exactly 36.
All inputs are finite; a program needn't handle non-finite values.
Results may differ from the reference program's by a relative error of at most 0.009.
Values may be sent and summed in bfloat16 or wider, within the bound.
A program may use at most 128 MiB of HBM per device.

```python
import math
import jax
import jax.numpy as jnp
import numpy as np
from jax import lax

D = 3584
FF = 1024
TOPK = 8
RANK = 128
TOK_DEV = 64
EXPERTS = 16
TOKENS = 1024
CAP = 36
FF_DEV = 512
N_DP = 2


def block_scale(rng, shape, cuts, smallest, largest):
    factor_of = 1.0
    for axis_at, shards_of in cuts:
        steps = jax.random.uniform(jax.random.fold_in(jax.random.fold_in(rng, 6), axis_at), (shards_of,), jnp.float32, smallest / len(cuts), largest / len(cuts))
        factor_of = factor_of * jnp.repeat(jnp.exp(steps), shape[axis_at] // shards_of).reshape((-1,) + (1,) * (len(shape) - 1 - axis_at))
    return factor_of


def routed_block(stream_key, own, number, rows, count, top, limit, slope):
    sequence = jax.random.permutation(stream_key, count)
    crowded, ordinary = load_shares(count, rows * top, limit, slope, True), load_shares(count, rows * top, limit, slope, False)
    places = jnp.arange(count)

    def named(tallies, offset_by):
        used = int((tallies > 0).sum())
        fixed = max(1, used // 4)
        moved = fixed + (places - fixed + offset_by * (used - fixed)) % max(1, count - fixed)
        return jnp.zeros((count,), jnp.int32).at[sequence[jnp.where(places < fixed, places, moved)]].set(jnp.asarray(tallies, jnp.int32))

    tallies = jnp.where(number % 4 == 0, named(crowded, number // 4), named(ordinary, number - number // 4 - 1))
    mixed = jax.random.permutation(jax.random.fold_in(own, 3), count)
    donor, receiver = mixed[0:count // 2 * 2:2], mixed[1:count // 2 * 2:2]
    room = jnp.minimum(tallies[donor] - 1, limit - tallies[receiver]) // 2
    room = jnp.where((donor == sequence[0]) | (receiver == sequence[0]) | (tallies[receiver] == 0), 0, jnp.maximum(room, 0))
    moved = jax.random.randint(jax.random.fold_in(own, 4), (count // 2,), 0, 1 << 20) % (room + 1)
    tallies = tallies.at[donor].add(-moved).at[receiver].add(moved)
    items = jnp.searchsorted(jnp.cumsum(tallies), jnp.arange(rows * top), side="right").astype(jnp.int32)
    grid = items.reshape(top, rows).T
    grid = grid[jax.random.permutation(jax.random.fold_in(own, 1), rows)]
    offset_by = jax.random.randint(jax.random.fold_in(own, 2), (rows, 1), 0, top)
    return jnp.take_along_axis(grid, (jnp.arange(top)[None, :] + offset_by) % top, axis=1)


def load_shares(count, total, limit, lean, full):
    portions = [(1 << 20) // math.isqrt(grade ** lean) + 1 for grade in range(1, count + 1)]
    largest = limit if full else min(limit, max(-(-total // count), total * portions[0] // sum(portions)))
    least = 1 if total - largest >= count - 1 else 0
    given, spare = [largest] + [least] * (count - 1), total - largest - least * (count - 1)
    while spare > 0:
        free = [i for i in range(1, count) if given[i] < largest] or [i for i in range(1, count) if given[i] < limit]
        whole, budget = sum([portions[i] for i in free]), spare
        for i in free:
            extra = min(limit - given[i], max(1, budget * portions[i] // whole), spare)
            given[i] = given[i] + extra
            spare = spare - extra
    return np.array(given)


def gaussian(stream_key, dims, deviation, most, split=(), held_as=jnp.bfloat16):
    result = deviation * jax.random.normal(stream_key, dims, jnp.float32)
    if split:
        result = result * block_scale(stream_key, dims, split, -0.22, 0.18)
    return jnp.clip(result, -most, most).astype(held_as)


def setup_inputs(seed: int = 0) -> dict:
    streams_of = jax.random.split(jax.random.key(seed), 9)
    saved_inputs = gaussian(streams_of[0], (TOKENS, D), 1.0, 6.0, ((0, 16),))
    output_grad = gaussian(streams_of[1], (TOKENS, D), 1.0, 6.0, ((0, 16),))
    routes_keys = jax.random.split(jax.random.fold_in(streams_of[2], 1), TOKENS // TOK_DEV)
    routes_turns = jax.random.permutation(jax.random.fold_in(streams_of[2], 3), TOKENS // TOK_DEV)
    routes = jax.vmap(lambda own, number: routed_block(jax.random.fold_in(streams_of[2], 2), own, number, TOK_DEV, EXPERTS, TOPK, CAP, 2))(routes_keys, routes_turns).reshape((TOKENS, TOPK))
    route_gates = jnp.clip(jnp.exp(math.log(1.0) - 2.306499 * jax.random.uniform(streams_of[3], (TOKENS, TOPK), jnp.float32) ** block_scale(streams_of[3], (TOKENS, TOPK), ((0, 16),), -0.2, 0.2)), 0.099609375, 1.0).astype(jnp.bfloat16)
    expert_gate = gaussian(streams_of[4], (EXPERTS, D, FF), D ** -0.5, 0.09375, ((0, 16), (2, 2)))
    expert_up = gaussian(streams_of[5], (EXPERTS, D, FF), D ** -0.5, 0.09375, ((0, 16), (2, 2)))
    expert_down = gaussian(streams_of[6], (EXPERTS, FF, D), FF ** -0.5, 0.1875, ((0, 16), (1, 2)))
    proj_basis = gaussian(streams_of[7], (EXPERTS, FF, RANK), FF ** -0.5, 0.1875, ((0, 16), (1, 2)))
    return dict(saved_inputs=saved_inputs, output_grad=output_grad, routes=routes, route_gates=route_gates, expert_gate=expert_gate, expert_up=expert_up, expert_down=expert_down, proj_basis=proj_basis)


def reference(saved_inputs, output_grad, routes, route_gates, expert_gate, expert_up, expert_down, proj_basis):
    sources = EXPERTS
    flat_routes = routes.reshape(sources, TOK_DEV * TOPK)
    one_hot = (flat_routes[:, :, None] == jnp.arange(EXPERTS, dtype=jnp.int32)[None, None, :]).astype(jnp.int32)
    earlier = jnp.sum((jnp.cumsum(one_hot, axis=1) - one_hot) * one_hot, axis=2)
    source_ids = jnp.arange(sources, dtype=jnp.int32)[:, None]
    per_expert = sources * CAP
    target_row = (flat_routes * per_expert + source_ids * CAP + earlier).reshape(-1).astype(jnp.int32)
    token_ids = jnp.repeat(jnp.arange(TOKENS, dtype=jnp.int32), TOPK)
    total_rows = EXPERTS * per_expert
    input_rows = jnp.zeros((total_rows, D), jnp.bfloat16).at[target_row].set(saved_inputs[token_ids])
    grad_rows = jnp.zeros((total_rows, D), jnp.bfloat16).at[target_row].set(output_grad[token_ids])
    gate_rows = jnp.zeros((total_rows,), jnp.bfloat16).at[target_row].set(route_gates.reshape(-1))
    owner_rows = jnp.full((total_rows,), TOKENS, jnp.int32).at[target_row].set(token_ids)
    input_rows = input_rows.reshape(EXPERTS, per_expert, D)
    grad_rows = grad_rows.reshape(EXPERTS, per_expert, D)
    gate_rows = gate_rows.reshape(EXPERTS, per_expert)
    owner_rows = owner_rows.reshape(EXPERTS, per_expert)

    def expert_step(accum, items):
        xin, yin, gin, owners, gate_w, up_w, down_w, basis = items
        gain = gin.astype(jnp.float32)[:, None]
        part_total = jnp.zeros((per_expert, D), jnp.float32)
        terms = jnp.zeros((D, 3, RANK), jnp.float32)
        for block in range(N_DP):
            lower = block * FF_DEV
            gate_b = gate_w[:, lower:lower + FF_DEV]
            up_b = up_w[:, lower:lower + FF_DEV]
            down_b = down_w[lower:lower + FF_DEV, :]
            basis_b = basis[lower:lower + FF_DEV, :]
            pre_gate = jnp.dot(xin, gate_b, preferred_element_type=jnp.float32)
            pre_up = jnp.dot(xin, up_b, preferred_element_type=jnp.float32)
            grad_hidden = jnp.dot(yin, down_b.T, preferred_element_type=jnp.float32)
            sigma = jax.nn.sigmoid(pre_gate)
            silu_val = pre_gate * sigma
            scaled = gain * grad_hidden
            grad_up = (scaled * silu_val).astype(jnp.bfloat16)
            grad_gate = (scaled * pre_up * sigma * (1.0 + pre_gate * (1.0 - sigma))).astype(jnp.bfloat16)
            hidden = (silu_val * pre_up).astype(jnp.bfloat16)
            part_b = (jnp.dot(grad_gate, gate_b.T, preferred_element_type=jnp.float32)
                      + jnp.dot(grad_up, up_b.T, preferred_element_type=jnp.float32)).astype(jnp.bfloat16)
            part_total = part_total + part_b.astype(jnp.float32)
            coef_gate = jnp.dot(grad_gate, basis_b, preferred_element_type=jnp.float32).astype(jnp.bfloat16)
            coef_up = jnp.dot(grad_up, basis_b, preferred_element_type=jnp.float32).astype(jnp.bfloat16)
            coef_down = (gain * jnp.dot(hidden, basis_b, preferred_element_type=jnp.float32)).astype(jnp.bfloat16)
            term_b = jnp.stack([
                jnp.dot(xin.T, coef_gate, preferred_element_type=jnp.float32),
                jnp.dot(xin.T, coef_up, preferred_element_type=jnp.float32),
                jnp.dot(yin.T, coef_down, preferred_element_type=jnp.float32)], axis=1).astype(jnp.bfloat16)
            terms = terms + term_b.astype(jnp.float32)
        accum = accum.at[owners].add(part_total, mode="drop")
        return accum, terms

    start_grad = jnp.zeros((TOKENS, D), jnp.float32)
    grads, projected = lax.scan(expert_step, start_grad, (input_rows, grad_rows, gate_rows, owner_rows, expert_gate, expert_up, expert_down, proj_basis))
    return grads.astype(jnp.bfloat16), projected
```

```python
import jax
import jax.numpy as jnp
from jax import lax
from jax.sharding import PartitionSpec as P


def slot_form(
    saved_inputs, output_grad, routes, route_gates, expert_gate, expert_up, expert_down, proj_basis
):
    token_count, model_width = saved_inputs.shape
    top_count = routes.shape[1]
    expert_count = lax.axis_size("expert")
    group_count = lax.axis_size("dp")
    capacity = token_count * top_count * 9 // (8 * expert_count)
    slot_count = expert_count * capacity
    column_width = model_width // group_count
    route_count = token_count * top_count
    flat_routes = routes.reshape(-1)
    one_hot = (flat_routes[:, None] == jnp.arange(expert_count, dtype=jnp.int32)[None, :]).astype(
        jnp.int32
    )
    earlier = jnp.sum((jnp.cumsum(one_hot, axis=0) - one_hot) * one_hot, axis=1)
    target_slot = flat_routes * capacity + earlier
    slot_owner = (
        jnp.full((slot_count,), route_count, jnp.int32)
        .at[target_slot]
        .set(jnp.arange(route_count, dtype=jnp.int32))
    )
    filled = slot_owner < route_count
    safe_route = jnp.minimum(slot_owner, route_count - 1)
    source_token = safe_route // top_count
    zero_half = jnp.zeros((), jnp.bfloat16)
    gate_slots = jnp.where(filled, route_gates.reshape(-1)[safe_route], zero_half).reshape(
        expert_count, capacity
    )
    token_map = (
        (source_token[None, :] == jnp.arange(token_count, dtype=jnp.int32)[:, None])
        & filled[None, :]
    ).astype(jnp.bfloat16)
    contract_first = (((0,), (0,)), ((), ()))

    def to_slots(source_rows):
        picked = lax.dot_general(
            token_map, source_rows, contract_first, preferred_element_type=jnp.float32
        ).astype(jnp.bfloat16)
        return picked.reshape(expert_count, capacity * source_rows.shape[1])

    recv_inputs, recv_grads, recv_gates = (
        lax.all_to_all(to_slots(saved_inputs), "expert", split_axis=0, concat_axis=0, tiled=True),
        lax.all_to_all(to_slots(output_grad), "expert", split_axis=0, concat_axis=0, tiled=True),
        lax.all_to_all(gate_slots, "expert", split_axis=0, concat_axis=0, tiled=True),
    )
    input_rows = recv_inputs.reshape(slot_count, model_width)
    grad_rows = recv_grads.reshape(slot_count, model_width)
    gain = recv_gates.reshape(slot_count, 1).astype(jnp.float32)
    gate_w = expert_gate[0]
    up_w = expert_up[0]
    down_w = expert_down[0]
    basis = proj_basis[0]
    rank_width = basis.shape[1]
    contract_last = (((1,), (1,)), ((), ()))
    pre_gate = jnp.dot(input_rows, gate_w, preferred_element_type=jnp.float32)
    pre_up = jnp.dot(input_rows, up_w, preferred_element_type=jnp.float32)
    grad_hidden = lax.dot_general(
        grad_rows, down_w, contract_last, preferred_element_type=jnp.float32
    )
    sigma = jax.nn.sigmoid(pre_gate)
    silu_val = pre_gate * sigma
    scaled = gain * grad_hidden
    grad_up = (scaled * silu_val).astype(jnp.bfloat16)
    grad_gate = (scaled * pre_up * sigma * (1.0 + pre_gate * (1.0 - sigma))).astype(jnp.bfloat16)
    hidden = (silu_val * pre_up).astype(jnp.bfloat16)
    part_rows = (
        lax.dot_general(grad_gate, gate_w, contract_last, preferred_element_type=jnp.float32)
        + lax.dot_general(grad_up, up_w, contract_last, preferred_element_type=jnp.float32)
    ).astype(jnp.bfloat16)
    coef_gate = jnp.dot(grad_gate, basis, preferred_element_type=jnp.float32).astype(jnp.bfloat16)
    coef_up = jnp.dot(grad_up, basis, preferred_element_type=jnp.float32).astype(jnp.bfloat16)
    coef_down = (gain * jnp.dot(hidden, basis, preferred_element_type=jnp.float32)).astype(
        jnp.bfloat16
    )
    coef_pair = jnp.concatenate([coef_gate, coef_up], axis=1)
    front = lax.dot_general(
        input_rows, coef_pair, contract_first, preferred_element_type=jnp.float32
    )
    rear = lax.dot_general(grad_rows, coef_down, contract_first, preferred_element_type=jnp.float32)
    summed_terms = lax.psum_scatter(
        jnp.concatenate([front, rear], axis=1).astype(jnp.bfloat16),
        "dp",
        scatter_dimension=0,
        tiled=True,
    ).astype(jnp.float32)
    projected = summed_terms.reshape(1, column_width, 3, rank_width)
    returned = lax.all_to_all(
        part_rows.reshape(expert_count, capacity * model_width),
        "expert",
        split_axis=0,
        concat_axis=0,
        tiled=True,
    )
    spread = jnp.dot(
        token_map, returned.reshape(slot_count, model_width), preferred_element_type=jnp.float32
    )
    token_grad = lax.psum_scatter(
        spread.astype(jnp.bfloat16), "dp", scatter_dimension=1, tiled=True
    )
    return (token_grad, projected)


def dense_form(
    saved_inputs, output_grad, routes, route_gates, expert_gate, expert_up, expert_down, proj_basis
):
    model_width = saved_inputs.shape[1]
    expert_count = lax.axis_size("expert")
    group_count = lax.axis_size("dp")
    column_width = model_width // group_count
    experts = jnp.arange(expert_count, dtype=jnp.int32)
    chosen = routes[:, :, None] == experts[None, None, :]
    gate_table = jnp.sum(
        jnp.where(chosen, route_gates.astype(jnp.float32)[:, :, None], 0.0), axis=1
    ).astype(jnp.bfloat16)
    all_gates = lax.all_gather(gate_table, "expert", axis=0, tiled=True)
    input_rows = lax.all_gather(saved_inputs, "expert", axis=0, tiled=True)
    grad_rows = lax.all_gather(output_grad, "expert", axis=0, tiled=True)
    own = experts == lax.axis_index("expert")
    gain = jnp.sum(
        jnp.where(own[None, :], all_gates.astype(jnp.float32), 0.0), axis=1, keepdims=True
    )
    gate_w = expert_gate[0]
    up_w = expert_up[0]
    down_w = expert_down[0]
    basis = proj_basis[0]
    rank_width = basis.shape[1]
    contract_first = (((0,), (0,)), ((), ()))
    contract_last = (((1,), (1,)), ((), ()))
    pre_gate = jnp.dot(input_rows, gate_w, preferred_element_type=jnp.float32)
    pre_up = jnp.dot(input_rows, up_w, preferred_element_type=jnp.float32)
    grad_hidden = lax.dot_general(
        grad_rows, down_w, contract_last, preferred_element_type=jnp.float32
    )
    sigma = jax.nn.sigmoid(pre_gate)
    silu_val = pre_gate * sigma
    scaled = gain * grad_hidden
    grad_up = (scaled * silu_val).astype(jnp.bfloat16)
    grad_gate = (scaled * pre_up * sigma * (1.0 + pre_gate * (1.0 - sigma))).astype(jnp.bfloat16)
    hidden = (silu_val * pre_up).astype(jnp.bfloat16)
    part_rows = (
        lax.dot_general(grad_gate, gate_w, contract_last, preferred_element_type=jnp.float32)
        + lax.dot_general(grad_up, up_w, contract_last, preferred_element_type=jnp.float32)
    ).astype(jnp.bfloat16)
    own_rows = lax.psum_scatter(part_rows, "expert", scatter_dimension=0, tiled=True)
    token_grad = lax.psum_scatter(own_rows, "dp", scatter_dimension=1, tiled=True)
    coef_gate = jnp.dot(grad_gate, basis, preferred_element_type=jnp.float32).astype(jnp.bfloat16)
    coef_up = jnp.dot(grad_up, basis, preferred_element_type=jnp.float32).astype(jnp.bfloat16)
    coef_down = (gain * jnp.dot(hidden, basis, preferred_element_type=jnp.float32)).astype(
        jnp.bfloat16
    )
    coef_pair = jnp.concatenate([coef_gate, coef_up], axis=1)
    front = lax.dot_general(
        input_rows, coef_pair, contract_first, preferred_element_type=jnp.float32
    )
    rear = lax.dot_general(grad_rows, coef_down, contract_first, preferred_element_type=jnp.float32)
    summed_terms = lax.psum_scatter(
        jnp.concatenate([front, rear], axis=1).astype(jnp.bfloat16),
        "dp",
        scatter_dimension=0,
        tiled=True,
    ).astype(jnp.float32)
    projected = summed_terms.reshape(1, column_width, 3, rank_width)
    return (token_grad, projected)


def on_device(*arrays):
    if lax.axis_size("expert") <= 2 * arrays[2].shape[1]:
        return dense_form(*arrays)
    return slot_form(*arrays)


def solution(mesh):
    placed = (
        P("expert", None),
        P("expert", None),
        P("expert", None),
        P("expert", None),
        P("expert", None, "dp"),
        P("expert", None, "dp"),
        P("expert", "dp", None),
        P("expert", "dp", None),
    )
    return jax.shard_map(
        on_device,
        mesh=mesh,
        in_specs=placed,
        out_specs=(P("expert", "dp"), P("expert", "dp", None, None)),
        check_vma=False,
    )
```

```python
import functools

import jax
import jax.numpy as jnp
from jax import lax
from jax.experimental import pallas as pl
from jax.experimental.pallas import tpu as pltpu
from jax.sharding import PartitionSpec as P


def slot_form(
    saved_inputs, output_grad, routes, route_gates, expert_gate, expert_up, expert_down, proj_basis
):
    token_count, model_width = saved_inputs.shape
    top_count = routes.shape[1]
    expert_count = lax.axis_size("expert")
    group_count = lax.axis_size("dp")
    capacity = token_count * top_count * 9 // (8 * expert_count)
    slot_count = expert_count * capacity
    column_width = model_width // group_count
    route_count = token_count * top_count
    flat_routes = routes.reshape(-1)
    one_hot = (flat_routes[:, None] == jnp.arange(expert_count, dtype=jnp.int32)[None, :]).astype(
        jnp.int32
    )
    earlier = jnp.sum((jnp.cumsum(one_hot, axis=0) - one_hot) * one_hot, axis=1)
    target_slot = flat_routes * capacity + earlier
    slot_owner = (
        jnp.full((slot_count,), route_count, jnp.int32)
        .at[target_slot]
        .set(jnp.arange(route_count, dtype=jnp.int32))
    )
    filled = slot_owner < route_count
    safe_route = jnp.minimum(slot_owner, route_count - 1)
    source_token = safe_route // top_count
    zero_half = jnp.zeros((), jnp.bfloat16)
    gate_slots = jnp.where(filled, route_gates.reshape(-1)[safe_route], zero_half).reshape(
        expert_count, capacity
    )
    token_map = (
        (source_token[None, :] == jnp.arange(token_count, dtype=jnp.int32)[:, None])
        & filled[None, :]
    ).astype(jnp.bfloat16)
    contract_first = (((0,), (0,)), ((), ()))

    def to_slots(source_rows):
        picked = lax.dot_general(
            token_map, source_rows, contract_first, preferred_element_type=jnp.float32
        ).astype(jnp.bfloat16)
        return picked.reshape(expert_count, capacity * source_rows.shape[1])

    recv_inputs, recv_grads, recv_gates = (
        lax.all_to_all(to_slots(saved_inputs), "expert", split_axis=0, concat_axis=0, tiled=True),
        lax.all_to_all(to_slots(output_grad), "expert", split_axis=0, concat_axis=0, tiled=True),
        lax.all_to_all(gate_slots, "expert", split_axis=0, concat_axis=0, tiled=True),
    )
    input_rows = recv_inputs.reshape(slot_count, model_width)
    grad_rows = recv_grads.reshape(slot_count, model_width)
    gain = recv_gates.reshape(slot_count, 1).astype(jnp.float32)
    gate_w = expert_gate[0]
    up_w = expert_up[0]
    down_w = expert_down[0]
    basis = proj_basis[0]
    rank_width = basis.shape[1]
    contract_last = (((1,), (1,)), ((), ()))
    pre_gate = jnp.dot(input_rows, gate_w, preferred_element_type=jnp.float32)
    pre_up = jnp.dot(input_rows, up_w, preferred_element_type=jnp.float32)
    grad_hidden = lax.dot_general(
        grad_rows, down_w, contract_last, preferred_element_type=jnp.float32
    )
    sigma = jax.nn.sigmoid(pre_gate)
    silu_val = pre_gate * sigma
    scaled = gain * grad_hidden
    grad_up = (scaled * silu_val).astype(jnp.bfloat16)
    grad_gate = (scaled * pre_up * sigma * (1.0 + pre_gate * (1.0 - sigma))).astype(jnp.bfloat16)
    hidden = (silu_val * pre_up).astype(jnp.bfloat16)
    part_rows = (
        lax.dot_general(grad_gate, gate_w, contract_last, preferred_element_type=jnp.float32)
        + lax.dot_general(grad_up, up_w, contract_last, preferred_element_type=jnp.float32)
    ).astype(jnp.bfloat16)
    coef_gate = jnp.dot(grad_gate, basis, preferred_element_type=jnp.float32).astype(jnp.bfloat16)
    coef_up = jnp.dot(grad_up, basis, preferred_element_type=jnp.float32).astype(jnp.bfloat16)
    coef_down = (gain * jnp.dot(hidden, basis, preferred_element_type=jnp.float32)).astype(
        jnp.bfloat16
    )
    coef_pair = jnp.concatenate([coef_gate, coef_up], axis=1)
    front = lax.dot_general(
        input_rows, coef_pair, contract_first, preferred_element_type=jnp.float32
    )
    rear = lax.dot_general(grad_rows, coef_down, contract_first, preferred_element_type=jnp.float32)
    summed_terms = lax.psum_scatter(
        jnp.concatenate([front, rear], axis=1).astype(jnp.bfloat16),
        "dp",
        scatter_dimension=0,
        tiled=True,
    ).astype(jnp.float32)
    projected = summed_terms.reshape(1, column_width, 3, rank_width)
    returned = lax.all_to_all(
        part_rows.reshape(expert_count, capacity * model_width),
        "expert",
        split_axis=0,
        concat_axis=0,
        tiled=True,
    )
    spread = jnp.dot(
        token_map, returned.reshape(slot_count, model_width), preferred_element_type=jnp.float32
    )
    token_grad = lax.psum_scatter(
        spread.astype(jnp.bfloat16), "dp", scatter_dimension=1, tiled=True
    )
    return (token_grad, projected)

MESH = pl.DeviceIdType.MESH
LANES = 128


def gather_kernel(
    depth, split, x_in, y_in, g_in, x_all, y_all, g_all,
    x_hold, y_hold, g_hold, recv_sem, up_sem, down_sem, side_sem, plane_sem, core_sem, local_sem,
):
    dp = lax.axis_index("dp")
    me = lax.axis_index("expert")
    z, y, core = me // 4, (me // 2) % 2, me % 2
    rows, width = x_in.shape
    own_cols = pl.ds(pl.multiple_of(dp * split, LANES), split)
    far_cols = pl.ds(pl.multiple_of((1 - dp) * split, LANES), split)
    rest_cols = pl.ds(2 * split, width - 2 * split)
    all_cols = pl.ds(0, g_in.shape[1])
    pieces = (
        (x_in, x_all, own_cols), (y_in, y_all, own_cols),
        (x_in, x_all, rest_cols), (y_in, y_all, rest_cols),
        (g_in, g_all, all_cols),
        (x_in, x_all, far_cols), (y_in, y_all, far_cols),
    )
    planar = range(5)

    def index(zz, yy, cc):
        return zz * 4 + yy * 2 + cc

    def landed(piece, item):
        _, whole, cols = pieces[piece]
        return whole.at[pl.ds(pl.multiple_of(item * rows, rows), rows), cols]

    def copy(piece, item, own, sem, device, recv_piece):
        start, _, cols = pieces[piece]
        src = start.at[:, cols] if own else landed(piece, item)
        return pltpu.make_async_remote_copy(
            src_ref=src,
            dst_ref=landed(piece, item),
            send_sem=sem,
            recv_sem=recv_sem.at[recv_piece, item],
            device_id=device,
            device_id_type=MESH,
        )

    def up(piece, zz, own=False):
        return copy(piece, index(zz, y, core), own, up_sem.at[piece, zz], (dp, me + 4), piece)

    def down(piece, zz, own=False):
        return copy(piece, index(zz, y, core), own, down_sem.at[piece, zz], (dp, me - 4), piece)

    def side(piece, zz, own=False):
        partner = index(z, 1 - y, core)
        return copy(piece, index(zz, y, core), own, side_sem.at[piece, zz], (dp, partner), piece)

    def plane(piece, zz, yy):
        item = index(zz, yy, core)
        return copy(piece, item, False, plane_sem.at[piece, item // 2], (1 - dp, me), piece + 5)

    def other(piece, zz, yy, own=False):
        item = index(zz, yy, core)
        partner = index(z, y, 1 - core)
        return copy(piece, item, own, core_sem.at[piece, item // 2], (dp, partner), piece)

    def arrive(piece, item):
        copy(piece, item, False, core_sem.at[0, 0], (dp, me), piece).wait_recv()

    barrier = pltpu.get_barrier_semaphore()

    def greet(device):
        pl.semaphore_signal(barrier, inc=1, device_id=device, device_id_type=MESH)

    greet((1 - dp, me))
    greet((dp, index(z, 1 - y, core)))
    greet((dp, index(z, y, 1 - core)))
    pl.when(z > 0)(lambda: greet((dp, me - 4)))
    pl.when(z < depth - 1)(lambda: greet((dp, me + 4)))
    pl.semaphore_wait(barrier, 3 + jnp.minimum(z, 1) + jnp.minimum(depth - 1 - z, 1))

    for piece in planar:
        pl.when(z < depth - 1)(lambda piece=piece: up(piece, z, True).start())
        pl.when(z > 0)(lambda piece=piece: down(piece, z, True).start())
        side(piece, z, True).start()
    for piece in range(7):
        other(piece, z, y, True).start()
    mine = pl.ds(pl.multiple_of(me * rows, rows), rows)
    holds = ((x_in, x_hold, x_all), (y_in, y_hold, y_all), (g_in, g_hold, g_all))
    into = [pltpu.make_async_copy(a, b, local_sem.at[i]) for i, (a, b, _) in enumerate(holds)]
    out = [
        pltpu.make_async_copy(b, c.at[mine], local_sem.at[3 + i])
        for i, (_, b, c) in enumerate(holds)
    ]
    for one in into:
        one.start()
    for one, two in zip(into, out):
        one.wait()
        two.start()

    def spots(away):
        if away == 0:
            return [(z, None)]
        return [(z - away, z >= away), (z + away, z + away < depth)]

    def guarded(condition, act):
        act() if condition is None else pl.when(condition)(act)

    def along_z(piece, zz, from_below):
        def act():
            arrive(piece, index(zz, y, core))
            if from_below:
                pl.when(z < depth - 1)(lambda: up(piece, zz).start())
            else:
                pl.when(z > 0)(lambda: down(piece, zz).start())
            side(piece, zz).start()
            if piece < 2:
                plane(piece, zz, y).start()
            other(piece, zz, y).start()
        return act

    def from_side(piece, zz):
        def act():
            arrive(piece, index(zz, 1 - y, core))
            if piece < 2:
                plane(piece, zz, 1 - y).start()
            other(piece, zz, 1 - y).start()
        return act

    def from_plane(piece, zz, yy):
        def act():
            arrive(piece, index(zz, yy, core))
            other(piece, zz, yy).start()
        return act

    for step in range(1, depth + 2):
        for piece in planar:
            if step < depth:
                for below, (zz, there) in zip((True, False), spots(step)):
                    guarded(there, along_z(piece, zz, below))
            if step <= depth:
                for zz, there in spots(step - 1):
                    guarded(there, from_side(piece, zz))
        for piece in (5, 6):
            if 1 <= step - 1 < depth:
                for zz, there in spots(step - 1):
                    guarded(there, from_plane(piece, zz, y))
            if step >= 2:
                for zz, there in spots(step - 2):
                    guarded(there, from_plane(piece, zz, 1 - y))

    for piece in range(7):
        for pair in range(2 * depth):
            arrive(piece, pair * 2 + 1 - core)
    for piece in planar:
        for zz in range(depth):
            pl.when((zz <= z) & (z < depth - 1))(lambda p=piece, q=zz: up(p, q).wait_send())
            pl.when((zz >= z) & (z > 0))(lambda p=piece, q=zz: down(p, q).wait_send())
            side(piece, zz).wait_send()
    for piece in range(2):
        for pair in range(2 * depth):
            pl.when(pair != me // 2)(
                lambda p=piece, q=pair: plane(p, q // 2, q % 2).wait_send()
            )
    for piece in range(7):
        for pair in range(2 * depth):
            other(piece, pair // 2, pair % 2).wait_send()
    for one in out:
        one.wait()


def gather_rows(saved_inputs, output_grad, gate_table):
    expert_count = lax.axis_size("expert")
    rows, width = saved_inputs.shape
    depth = expert_count // 4
    split = width * 5 // 14 // LANES * LANES
    gate_width = gate_table.shape[1]
    dma = pltpu.SemaphoreType.DMA
    whole = pl.BlockSpec(memory_space=pl.ANY)
    return pl.pallas_call(
        functools.partial(gather_kernel, depth, split),
        out_shape=[
            jax.ShapeDtypeStruct((expert_count * rows, width), jnp.bfloat16),
            jax.ShapeDtypeStruct((expert_count * rows, width), jnp.bfloat16),
            jax.ShapeDtypeStruct((expert_count * rows, gate_width), jnp.bfloat16),
        ],
        in_specs=[whole] * 3,
        out_specs=[whole] * 3,
        scratch_shapes=[
            pltpu.VMEM((rows, width), jnp.bfloat16),
            pltpu.VMEM((rows, width), jnp.bfloat16),
            pltpu.VMEM((rows, gate_width), jnp.bfloat16),
            dma((7, expert_count)),
            dma((5, depth)),
            dma((5, depth)),
            dma((5, depth)),
            dma((2, 2 * depth)),
            dma((7, 2 * depth)),
            dma((6,)),
        ],
        compiler_params=pltpu.CompilerParams(collective_id=0, has_side_effects=True),
    )(saved_inputs, output_grad, gate_table)


def dense_form(
    saved_inputs, output_grad, routes, route_gates, expert_gate, expert_up, expert_down, proj_basis
):
    model_width = saved_inputs.shape[1]
    group_count = lax.axis_size("dp")
    column_width = model_width // group_count
    experts = jnp.arange(LANES, dtype=jnp.int32)
    chosen = routes[:, :, None] == experts[None, None, :]
    gate_table = jnp.sum(
        jnp.where(chosen, route_gates.astype(jnp.float32)[:, :, None], 0.0), axis=1
    ).astype(jnp.bfloat16)
    input_rows, grad_rows, all_gates = gather_rows(saved_inputs, output_grad, gate_table)
    own = experts == lax.axis_index("expert")
    gain = jnp.sum(
        jnp.where(own[None, :], all_gates.astype(jnp.float32), 0.0), axis=1, keepdims=True
    )
    gate_w = expert_gate[0]
    up_w = expert_up[0]
    down_w = expert_down[0]
    basis = proj_basis[0]
    rank_width = basis.shape[1]
    contract_first = (((0,), (0,)), ((), ()))
    contract_last = (((1,), (1,)), ((), ()))
    pre_gate = jnp.dot(input_rows, gate_w, preferred_element_type=jnp.float32)
    pre_up = jnp.dot(input_rows, up_w, preferred_element_type=jnp.float32)
    grad_hidden = lax.dot_general(
        grad_rows, down_w, contract_last, preferred_element_type=jnp.float32
    )
    sigma = jax.nn.sigmoid(pre_gate)
    silu_val = pre_gate * sigma
    scaled = gain * grad_hidden
    grad_up = (scaled * silu_val).astype(jnp.bfloat16)
    grad_gate = (scaled * pre_up * sigma * (1.0 + pre_gate * (1.0 - sigma))).astype(jnp.bfloat16)
    hidden = (silu_val * pre_up).astype(jnp.bfloat16)
    part_rows = (
        lax.dot_general(grad_gate, gate_w, contract_last, preferred_element_type=jnp.float32)
        + lax.dot_general(grad_up, up_w, contract_last, preferred_element_type=jnp.float32)
    ).astype(jnp.bfloat16)
    own_rows = lax.psum_scatter(part_rows, "expert", scatter_dimension=0, tiled=True)
    token_grad = lax.psum_scatter(own_rows, "dp", scatter_dimension=1, tiled=True)
    coef_gate = jnp.dot(grad_gate, basis, preferred_element_type=jnp.float32).astype(jnp.bfloat16)
    coef_up = jnp.dot(grad_up, basis, preferred_element_type=jnp.float32).astype(jnp.bfloat16)
    coef_down = (gain * jnp.dot(hidden, basis, preferred_element_type=jnp.float32)).astype(
        jnp.bfloat16
    )
    coef_pair = jnp.concatenate([coef_gate, coef_up], axis=1)
    front = lax.dot_general(
        input_rows, coef_pair, contract_first, preferred_element_type=jnp.float32
    )
    rear = lax.dot_general(grad_rows, coef_down, contract_first, preferred_element_type=jnp.float32)
    summed_terms = lax.psum_scatter(
        jnp.concatenate([front, rear], axis=1).astype(jnp.bfloat16),
        "dp",
        scatter_dimension=0,
        tiled=True,
    ).astype(jnp.float32)
    projected = summed_terms.reshape(1, column_width, 3, rank_width)
    return (token_grad, projected)


def on_device(*arrays):
    if lax.axis_size("expert") <= 2 * arrays[2].shape[1]:
        return dense_form(*arrays)
    return slot_form(*arrays)


def solution(mesh):
    placed = (
        P("expert", None),
        P("expert", None),
        P("expert", None),
        P("expert", None),
        P("expert", None, "dp"),
        P("expert", None, "dp"),
        P("expert", "dp", None),
        P("expert", "dp", None),
    )
    return jax.shard_map(
        on_device,
        mesh=mesh,
        in_specs=placed,
        out_specs=(P("expert", "dp"), P("expert", "dp", None, None)),
        check_vma=False,
    )
```

```python
import functools

import jax
import jax.numpy as jnp
from jax import lax
from jax.experimental import pallas as pl
from jax.experimental.pallas import tpu as pltpu
from jax.sharding import PartitionSpec as P


def slot_form(
    saved_inputs, output_grad, routes, route_gates, expert_gate, expert_up, expert_down, proj_basis
):
    token_count, model_width = saved_inputs.shape
    top_count = routes.shape[1]
    expert_count = lax.axis_size("expert")
    group_count = lax.axis_size("dp")
    capacity = token_count * top_count * 9 // (8 * expert_count)
    slot_count = expert_count * capacity
    column_width = model_width // group_count
    route_count = token_count * top_count
    flat_routes = routes.reshape(-1)
    one_hot = (flat_routes[:, None] == jnp.arange(expert_count, dtype=jnp.int32)[None, :]).astype(
        jnp.int32
    )
    earlier = jnp.sum((jnp.cumsum(one_hot, axis=0) - one_hot) * one_hot, axis=1)
    target_slot = flat_routes * capacity + earlier
    slot_owner = (
        jnp.full((slot_count,), route_count, jnp.int32)
        .at[target_slot]
        .set(jnp.arange(route_count, dtype=jnp.int32))
    )
    filled = slot_owner < route_count
    safe_route = jnp.minimum(slot_owner, route_count - 1)
    source_token = safe_route // top_count
    zero_half = jnp.zeros((), jnp.bfloat16)
    gate_slots = jnp.where(filled, route_gates.reshape(-1)[safe_route], zero_half).reshape(
        expert_count, capacity
    )
    token_map = (
        (source_token[None, :] == jnp.arange(token_count, dtype=jnp.int32)[:, None])
        & filled[None, :]
    ).astype(jnp.bfloat16)
    contract_first = (((0,), (0,)), ((), ()))

    def to_slots(source_rows):
        picked = lax.dot_general(
            token_map, source_rows, contract_first, preferred_element_type=jnp.float32
        ).astype(jnp.bfloat16)
        return picked.reshape(expert_count, capacity * source_rows.shape[1])

    recv_inputs, recv_grads, recv_gates = (
        lax.all_to_all(to_slots(saved_inputs), "expert", split_axis=0, concat_axis=0, tiled=True),
        lax.all_to_all(to_slots(output_grad), "expert", split_axis=0, concat_axis=0, tiled=True),
        lax.all_to_all(gate_slots, "expert", split_axis=0, concat_axis=0, tiled=True),
    )
    input_rows = recv_inputs.reshape(slot_count, model_width)
    grad_rows = recv_grads.reshape(slot_count, model_width)
    gain = recv_gates.reshape(slot_count, 1).astype(jnp.float32)
    gate_w = expert_gate[0]
    up_w = expert_up[0]
    down_w = expert_down[0]
    basis = proj_basis[0]
    rank_width = basis.shape[1]
    contract_last = (((1,), (1,)), ((), ()))
    pre_gate = jnp.dot(input_rows, gate_w, preferred_element_type=jnp.float32)
    pre_up = jnp.dot(input_rows, up_w, preferred_element_type=jnp.float32)
    grad_hidden = lax.dot_general(
        grad_rows, down_w, contract_last, preferred_element_type=jnp.float32
    )
    sigma = jax.nn.sigmoid(pre_gate)
    silu_val = pre_gate * sigma
    scaled = gain * grad_hidden
    grad_up = (scaled * silu_val).astype(jnp.bfloat16)
    grad_gate = (scaled * pre_up * sigma * (1.0 + pre_gate * (1.0 - sigma))).astype(jnp.bfloat16)
    hidden = (silu_val * pre_up).astype(jnp.bfloat16)
    part_rows = (
        lax.dot_general(grad_gate, gate_w, contract_last, preferred_element_type=jnp.float32)
        + lax.dot_general(grad_up, up_w, contract_last, preferred_element_type=jnp.float32)
    ).astype(jnp.bfloat16)
    coef_gate = jnp.dot(grad_gate, basis, preferred_element_type=jnp.float32).astype(jnp.bfloat16)
    coef_up = jnp.dot(grad_up, basis, preferred_element_type=jnp.float32).astype(jnp.bfloat16)
    coef_down = (gain * jnp.dot(hidden, basis, preferred_element_type=jnp.float32)).astype(
        jnp.bfloat16
    )
    coef_pair = jnp.concatenate([coef_gate, coef_up], axis=1)
    front = lax.dot_general(
        input_rows, coef_pair, contract_first, preferred_element_type=jnp.float32
    )
    rear = lax.dot_general(grad_rows, coef_down, contract_first, preferred_element_type=jnp.float32)
    summed_terms = lax.psum_scatter(
        jnp.concatenate([front, rear], axis=1).astype(jnp.bfloat16),
        "dp",
        scatter_dimension=0,
        tiled=True,
    ).astype(jnp.float32)
    projected = summed_terms.reshape(1, column_width, 3, rank_width)
    returned = lax.all_to_all(
        part_rows.reshape(expert_count, capacity * model_width),
        "expert",
        split_axis=0,
        concat_axis=0,
        tiled=True,
    )
    spread = jnp.dot(
        token_map, returned.reshape(slot_count, model_width), preferred_element_type=jnp.float32
    )
    token_grad = lax.psum_scatter(
        spread.astype(jnp.bfloat16), "dp", scatter_dimension=1, tiled=True
    )
    return (token_grad, projected)

MESH = pl.DeviceIdType.MESH
LANES = 128


def gather_kernel(
    depth, split, x_in, y_in, g_in, x_all, y_all, g_all,
    x_hold, y_hold, g_hold, recv_sem, up_sem, down_sem, side_sem, plane_sem, core_sem, local_sem,
):
    dp = lax.axis_index("dp")
    me = lax.axis_index("expert")
    z, y, core = me // 4, (me // 2) % 2, me % 2
    rows, width = x_in.shape
    own_cols = pl.ds(pl.multiple_of(dp * split, LANES), split)
    far_cols = pl.ds(pl.multiple_of((1 - dp) * split, LANES), split)
    rest_cols = pl.ds(2 * split, width - 2 * split)
    all_cols = pl.ds(0, g_in.shape[1])
    pieces = (
        (x_in, x_all, own_cols), (y_in, y_all, own_cols),
        (x_in, x_all, rest_cols), (y_in, y_all, rest_cols),
        (g_in, g_all, all_cols),
        (x_in, x_all, far_cols), (y_in, y_all, far_cols),
    )
    planar = range(5)

    def index(zz, yy, cc):
        return zz * 4 + yy * 2 + cc

    def landed(piece, item):
        _, whole, cols = pieces[piece]
        return whole.at[pl.ds(pl.multiple_of(item * rows, rows), rows), cols]

    def copy(piece, item, own, sem, device, recv_piece):
        start, _, cols = pieces[piece]
        src = start.at[:, cols] if own else landed(piece, item)
        return pltpu.make_async_remote_copy(
            src_ref=src,
            dst_ref=landed(piece, item),
            send_sem=sem,
            recv_sem=recv_sem.at[recv_piece, item],
            device_id=device,
            device_id_type=MESH,
        )

    def up(piece, zz, own=False):
        return copy(piece, index(zz, y, core), own, up_sem.at[piece, zz], (dp, me + 4), piece)

    def down(piece, zz, own=False):
        return copy(piece, index(zz, y, core), own, down_sem.at[piece, zz], (dp, me - 4), piece)

    def side(piece, zz, own=False):
        partner = index(z, 1 - y, core)
        return copy(piece, index(zz, y, core), own, side_sem.at[piece, zz], (dp, partner), piece)

    def plane(piece, zz, yy):
        item = index(zz, yy, core)
        return copy(piece, item, False, plane_sem.at[piece, item // 2], (1 - dp, me), piece + 5)

    def other(piece, zz, yy, own=False):
        item = index(zz, yy, core)
        partner = index(z, y, 1 - core)
        return copy(piece, item, own, core_sem.at[piece, item // 2], (dp, partner), piece)

    def arrive(piece, item):
        copy(piece, item, False, core_sem.at[0, 0], (dp, me), piece).wait_recv()

    barrier = pltpu.get_barrier_semaphore()

    def greet(device):
        pl.semaphore_signal(barrier, inc=1, device_id=device, device_id_type=MESH)

    greet((1 - dp, me))
    greet((dp, index(z, 1 - y, core)))
    greet((dp, index(z, y, 1 - core)))
    pl.when(z > 0)(lambda: greet((dp, me - 4)))
    pl.when(z < depth - 1)(lambda: greet((dp, me + 4)))
    pl.semaphore_wait(barrier, 3 + jnp.minimum(z, 1) + jnp.minimum(depth - 1 - z, 1))

    for piece in planar:
        pl.when(z < depth - 1)(lambda piece=piece: up(piece, z, True).start())
        pl.when(z > 0)(lambda piece=piece: down(piece, z, True).start())
        side(piece, z, True).start()
    for piece in range(7):
        other(piece, z, y, True).start()
    mine = pl.ds(pl.multiple_of(me * rows, rows), rows)
    holds = ((x_in, x_hold, x_all), (y_in, y_hold, y_all), (g_in, g_hold, g_all))
    into = [pltpu.make_async_copy(a, b, local_sem.at[i]) for i, (a, b, _) in enumerate(holds)]
    out = [
        pltpu.make_async_copy(b, c.at[mine], local_sem.at[3 + i])
        for i, (_, b, c) in enumerate(holds)
    ]
    for one in into:
        one.start()
    for one, two in zip(into, out):
        one.wait()
        two.start()

    def spots(away):
        if away == 0:
            return [(z, None)]
        return [(z - away, z >= away), (z + away, z + away < depth)]

    def guarded(condition, act):
        act() if condition is None else pl.when(condition)(act)

    def along_z(piece, zz, from_below):
        def act():
            arrive(piece, index(zz, y, core))
            if from_below:
                pl.when(z < depth - 1)(lambda: up(piece, zz).start())
            else:
                pl.when(z > 0)(lambda: down(piece, zz).start())
            side(piece, zz).start()
            if piece < 2:
                plane(piece, zz, y).start()
            other(piece, zz, y).start()
        return act

    def from_side(piece, zz):
        def act():
            arrive(piece, index(zz, 1 - y, core))
            if piece < 2:
                plane(piece, zz, 1 - y).start()
            other(piece, zz, 1 - y).start()
        return act

    def from_plane(piece, zz, yy):
        def act():
            arrive(piece, index(zz, yy, core))
            other(piece, zz, yy).start()
        return act

    for step in range(1, depth + 2):
        for piece in planar:
            if step < depth:
                for below, (zz, there) in zip((True, False), spots(step)):
                    guarded(there, along_z(piece, zz, below))
            if step <= depth:
                for zz, there in spots(step - 1):
                    guarded(there, from_side(piece, zz))
        for piece in (5, 6):
            if 1 <= step - 1 < depth:
                for zz, there in spots(step - 1):
                    guarded(there, from_plane(piece, zz, y))
            if step >= 2:
                for zz, there in spots(step - 2):
                    guarded(there, from_plane(piece, zz, 1 - y))

    for piece in range(7):
        for pair in range(2 * depth):
            arrive(piece, pair * 2 + 1 - core)
    for piece in planar:
        for zz in range(depth):
            pl.when((zz <= z) & (z < depth - 1))(lambda p=piece, q=zz: up(p, q).wait_send())
            pl.when((zz >= z) & (z > 0))(lambda p=piece, q=zz: down(p, q).wait_send())
            side(piece, zz).wait_send()
    for piece in range(2):
        for pair in range(2 * depth):
            pl.when(pair != me // 2)(
                lambda p=piece, q=pair: plane(p, q // 2, q % 2).wait_send()
            )
    for piece in range(7):
        for pair in range(2 * depth):
            other(piece, pair // 2, pair % 2).wait_send()
    for one in out:
        one.wait()


def gather_rows(saved_inputs, output_grad, gate_table):
    expert_count = lax.axis_size("expert")
    rows, width = saved_inputs.shape
    depth = expert_count // 4
    split = width * 5 // 14 // LANES * LANES
    gate_width = gate_table.shape[1]
    dma = pltpu.SemaphoreType.DMA
    whole = pl.BlockSpec(memory_space=pl.ANY)
    return pl.pallas_call(
        functools.partial(gather_kernel, depth, split),
        out_shape=[
            jax.ShapeDtypeStruct((expert_count * rows, width), jnp.bfloat16),
            jax.ShapeDtypeStruct((expert_count * rows, width), jnp.bfloat16),
            jax.ShapeDtypeStruct((expert_count * rows, gate_width), jnp.bfloat16),
        ],
        in_specs=[whole] * 3,
        out_specs=[whole] * 3,
        scratch_shapes=[
            pltpu.VMEM((rows, width), jnp.bfloat16),
            pltpu.VMEM((rows, width), jnp.bfloat16),
            pltpu.VMEM((rows, gate_width), jnp.bfloat16),
            dma((7, expert_count)),
            dma((5, depth)),
            dma((5, depth)),
            dma((5, depth)),
            dma((2, 2 * depth)),
            dma((7, 2 * depth)),
            dma((6,)),
        ],
        compiler_params=pltpu.CompilerParams(collective_id=0, has_side_effects=True),
    )(saved_inputs, output_grad, gate_table)


def scatter_kernel(
    depth, part, terms, grad_out, proj_out,
    mine, from_core, from_side, from_below, from_above, final, from_plane, own_terms, far_terms,
    local_sem, core_sem, side_sem, up_sem, down_sem, plane_sem, terms_sem,
):
    dp = lax.axis_index("dp")
    me = lax.axis_index("expert")
    z, y, core = me // 4, (me // 2) % 2, me % 2
    pairs = 2 * depth
    width = part.shape[3]
    chunk = width // 4
    order = (0, 2, 1, 3)
    core_device = (dp, z * 4 + y * 2 + 1 - core)
    side_device = (dp, z * 4 + (1 - y) * 2 + core)
    plane_device = (1 - dp, me)

    def cols(k):
        return pl.ds(k * chunk, chunk)

    def remote(src, dst, sems, device):
        return pltpu.make_async_remote_copy(
            src_ref=src, dst_ref=dst, send_sem=sems[0], recv_sem=sems[1],
            device_id=device, device_id_type=MESH,
        )

    def both(sem, *at):
        return sem.at[(0,) + at], sem.at[(1,) + at]

    def local_copy(k):
        return pltpu.make_async_copy(
            part.at[:, core, :, cols(k)], mine.at[:, :, cols(k)], local_sem.at[k]
        )

    def core_copy(k):
        return remote(
            part.at[:, 1 - core, :, cols(k)], from_core.at[:, :, cols(k)],
            both(core_sem, k), core_device,
        )

    def side_copy(k, zz):
        return remote(
            mine.at[zz * 2 + 1 - y, :, cols(k)], from_side.at[zz, :, cols(k)],
            both(side_sem, k, zz), side_device,
        )

    def up_copy(k, zz):
        return remote(
            mine.at[zz * 2 + y, :, cols(k)], from_below.at[zz, :, cols(k)],
            both(up_sem, k, zz), (dp, me + 4),
        )

    def down_copy(k, zz):
        return remote(
            mine.at[zz * 2 + y, :, cols(k)], from_above.at[zz, :, cols(k)],
            both(down_sem, k, zz), (dp, me - 4),
        )

    def plane_copy(k):
        return remote(
            final.at[:, cols(k)], from_plane.at[:, cols(k % 2)],
            both(plane_sem, k % 2), plane_device,
        )

    terms_copy = remote(terms.at[1 - dp], far_terms, both(terms_sem), plane_device)
    terms_local = pltpu.make_async_copy(terms.at[dp], own_terms, local_sem.at[4])

    barrier = pltpu.get_barrier_semaphore()

    def greet(device):
        pl.semaphore_signal(barrier, inc=1, device_id=device, device_id_type=MESH)

    greet(plane_device)
    greet(side_device)
    greet(core_device)
    pl.when(z > 0)(lambda: greet((dp, me - 4)))
    pl.when(z < depth - 1)(lambda: greet((dp, me + 4)))
    pl.semaphore_wait(barrier, 3 + jnp.minimum(z, 1) + jnp.minimum(depth - 1 - z, 1))

    for k in order:
        core_copy(k).start()
        local_copy(k).start()
    terms_copy.start()
    terms_local.start()

    def add_into(slot, k, other):
        total = mine[slot, :, cols(k)].astype(jnp.float32) + other.astype(jnp.float32)
        mine[slot, :, cols(k)] = total.astype(jnp.bfloat16)

    def over_cores(k):
        local_copy(k).wait()
        core_copy(k).wait_recv()
        for zz in range(depth):
            slot = zz * 2 + 1 - y
            add_into(slot, k, from_core[slot, :, cols(k)])
            side_copy(k, zz).start()
        for zz in range(depth):
            slot = zz * 2 + y
            add_into(slot, k, from_core[slot, :, cols(k)])

    def over_side(k):
        for zz in reversed(range(depth)):
            side_copy(k, zz).wait_recv()
            add_into(zz * 2 + y, k, from_side[zz, :, cols(k)])
            if zz > 0:
                pl.when(z == 0)(lambda zz=zz: up_copy(k, zz).start())
        for zz in range(depth - 1):
            pl.when(z == depth - 1)(lambda zz=zz: down_copy(k, zz).start())

    def along_z(k):
        for far in reversed(range(1, depth)):
            def rise(zz=far):
                up_copy(k, zz).wait_recv()
                add_into(zz * 2 + y, k, from_below[zz, :, cols(k)])
                up_copy(k, zz).start()

            def fall(zz=depth - 1 - far):
                down_copy(k, zz).wait_recv()
                add_into(zz * 2 + y, k, from_above[zz, :, cols(k)])
                down_copy(k, zz).start()

            pl.when((z > 0) & (z < far))(rise)
            pl.when((z < depth - 1) & (z > depth - 1 - far))(fall)

    def finish(k):
        slot = z * 2 + y

        def take_below():
            up_copy(k, z).wait_recv()
            add_into(slot, k, from_below[z, :, cols(k)])

        def take_above():
            down_copy(k, z).wait_recv()
            add_into(slot, k, from_above[z, :, cols(k)])

        pl.when(z > 0)(take_below)
        pl.when(z < depth - 1)(take_above)
        final[:, cols(k)] = mine[slot, :, cols(k)]
        pl.when(dp != k // 2)(lambda: plane_copy(k).start())

    stages = (over_cores, over_side, along_z, finish)
    for step in range(len(order) + len(stages) - 1):
        for number, stage in enumerate(stages):
            if 0 <= step - number < len(order):
                stage(order[step - number])

    terms_local.wait()
    terms_copy.wait()
    rank = proj_out.shape[2]
    for j in range(proj_out.shape[0]):
        at = pl.ds(j * rank, rank)
        proj_out[j] = own_terms[:, at].astype(jnp.float32) + far_terms[:, at].astype(jnp.float32)

    for k in range(4):
        def take_plane(k=k):
            plane_copy(k).wait_recv()
            total = final[:, cols(k)].astype(jnp.float32) + from_plane[:, cols(k % 2)].astype(
                jnp.float32
            )
            grad_out[:, cols(k % 2)] = total.astype(jnp.bfloat16)

        pl.when(dp == k // 2)(take_plane)
        pl.when(dp != k // 2)(lambda k=k: plane_copy(k).wait_send())
        core_copy(k).wait_send()
        for zz in range(depth):
            side_copy(k, zz).wait_send()
            pl.when(zz > z)(lambda k=k, zz=zz: up_copy(k, zz).wait_send())
            pl.when(zz < z)(lambda k=k, zz=zz: down_copy(k, zz).wait_send())


def scatter_sums(part_rows, terms, rank_width):
    group_count = lax.axis_size("dp")
    expert_count = lax.axis_size("expert")
    all_rows, width = part_rows.shape
    rows = all_rows // expert_count
    depth = expert_count // 4
    half = width // group_count
    columns = terms.shape[1]
    dma = pltpu.SemaphoreType.DMA
    whole = pl.BlockSpec(memory_space=pl.ANY)
    held = pl.BlockSpec(memory_space=pltpu.VMEM)
    half_type = jnp.bfloat16
    return pl.pallas_call(
        functools.partial(scatter_kernel, depth),
        out_shape=[
            jax.ShapeDtypeStruct((rows, half), half_type),
            jax.ShapeDtypeStruct((columns // rank_width, half, rank_width), jnp.float32),
        ],
        in_specs=[whole] * 2,
        out_specs=[held] * 2,
        scratch_shapes=[
            pltpu.VMEM((2 * depth, rows, width), half_type),
            pltpu.VMEM((2 * depth, rows, width), half_type),
            pltpu.VMEM((depth, rows, width), half_type),
            pltpu.VMEM((depth, rows, width), half_type),
            pltpu.VMEM((depth, rows, width), half_type),
            pltpu.VMEM((rows, width), half_type),
            pltpu.VMEM((rows, half), half_type),
            pltpu.VMEM((half, columns), half_type),
            pltpu.VMEM((half, columns), half_type),
            dma((5,)),
            dma((2, 4)),
            dma((2, 4, depth)),
            dma((2, 4, depth)),
            dma((2, 4, depth)),
            dma((2, 2)),
            dma((2,)),
        ],
        compiler_params=pltpu.CompilerParams(collective_id=1, has_side_effects=True),
    )(
        part_rows.reshape(2 * depth, 2, rows, width),
        terms.reshape(group_count, half, columns),
    )


def dense_form(
    saved_inputs, output_grad, routes, route_gates, expert_gate, expert_up, expert_down, proj_basis
):
    experts = jnp.arange(LANES, dtype=jnp.int32)
    chosen = routes[:, :, None] == experts[None, None, :]
    gate_table = jnp.sum(
        jnp.where(chosen, route_gates.astype(jnp.float32)[:, :, None], 0.0), axis=1
    ).astype(jnp.bfloat16)
    input_rows, grad_rows, all_gates = gather_rows(saved_inputs, output_grad, gate_table)
    own = experts == lax.axis_index("expert")
    gain = jnp.sum(
        jnp.where(own[None, :], all_gates.astype(jnp.float32), 0.0), axis=1, keepdims=True
    )
    gate_w = expert_gate[0]
    up_w = expert_up[0]
    down_w = expert_down[0]
    basis = proj_basis[0]
    rank_width = basis.shape[1]
    contract_first = (((0,), (0,)), ((), ()))
    contract_last = (((1,), (1,)), ((), ()))
    pre_gate = jnp.dot(input_rows, gate_w, preferred_element_type=jnp.float32)
    pre_up = jnp.dot(input_rows, up_w, preferred_element_type=jnp.float32)
    grad_hidden = lax.dot_general(
        grad_rows, down_w, contract_last, preferred_element_type=jnp.float32
    )
    sigma = jax.nn.sigmoid(pre_gate)
    silu_val = pre_gate * sigma
    scaled = gain * grad_hidden
    grad_up = (scaled * silu_val).astype(jnp.bfloat16)
    grad_gate = (scaled * pre_up * sigma * (1.0 + pre_gate * (1.0 - sigma))).astype(jnp.bfloat16)
    hidden = (silu_val * pre_up).astype(jnp.bfloat16)
    part_rows = (
        lax.dot_general(grad_gate, gate_w, contract_last, preferred_element_type=jnp.float32)
        + lax.dot_general(grad_up, up_w, contract_last, preferred_element_type=jnp.float32)
    ).astype(jnp.bfloat16)
    coef_gate = jnp.dot(grad_gate, basis, preferred_element_type=jnp.float32).astype(jnp.bfloat16)
    coef_up = jnp.dot(grad_up, basis, preferred_element_type=jnp.float32).astype(jnp.bfloat16)
    coef_down = (gain * jnp.dot(hidden, basis, preferred_element_type=jnp.float32)).astype(
        jnp.bfloat16
    )
    coef_pair = jnp.concatenate([coef_gate, coef_up], axis=1)
    front = lax.dot_general(
        input_rows, coef_pair, contract_first, preferred_element_type=jnp.float32
    )
    rear = lax.dot_general(grad_rows, coef_down, contract_first, preferred_element_type=jnp.float32)
    terms = jnp.concatenate([front, rear], axis=1).astype(jnp.bfloat16)
    token_grad, summed_terms = scatter_sums(part_rows, terms, rank_width)
    projected = summed_terms.transpose(1, 0, 2)[None]
    return (token_grad, projected)


def on_device(*arrays):
    if lax.axis_size("expert") <= 2 * arrays[2].shape[1]:
        return dense_form(*arrays)
    return slot_form(*arrays)


def solution(mesh):
    placed = (
        P("expert", None),
        P("expert", None),
        P("expert", None),
        P("expert", None),
        P("expert", None, "dp"),
        P("expert", None, "dp"),
        P("expert", "dp", None),
        P("expert", "dp", None),
    )
    return jax.shard_map(
        on_device,
        mesh=mesh,
        in_specs=placed,
        out_specs=(P("expert", "dp"), P("expert", "dp", None, None)),
        check_vma=False,
    )
```
